256 devices in a mesh: replica: 4 (over x_hi, core), fsdp: 64 (over z, y, x_lo).
Axes of the slice: x: 4 (x_hi: 2, x_lo: 2; x = x_hi * 2 + x_lo), y: 4, z: 8, core: 2. Of those that a mesh axis runs over, the one named last changes fastest.
Arguments:
- deltas: bfloat16 [4, 2, 2048, 16384], P('replica', None, 'fsdp'), may hold values from -3 to 3
- master: float32 [2, 2048, 16384], P(None, 'replica', 'fsdp'), may hold values from -3 to 3
- momentum: float32 [2, 2048, 16384], P(None, 'replica', 'fsdp'), may hold values from -2 to 2
Outputs:
- master_out: float32 [2, 2048, 16384], P(None, 'replica', 'fsdp')
- momentum_out: float32 [2, 2048, 16384], P(None, 'replica', 'fsdp')
- params_out: bfloat16 [2, 2048, 16384], P(None, 'fsdp')
The draws below stay inside these ranges and needn't reach their ends.
All inputs are finite; a program needn't handle non-finite values.
Results may differ from the reference program's by a relative error of at most 0.008.
Values may be sent and summed in bfloat16 or wider, within the bound.
No kernel may reach another device: no remote copies, remote signals or barrier semaphores. Data moves between devices by JAX's collectives and lax.ppermute only.
A program may use at most 64 MiB of HBM per device.

```python
import jax
import jax.numpy as jnp

D = 2048
FF = 16384
PROJ = 2
R = 4


def strengthened(result, own_key, source, target, shards_of, factor):
    def block_of(dim):
        return (jnp.arange(result.shape[dim]) // (result.shape[dim] // shards_of)).reshape((-1,) + (1,) * (result.ndim - 1 - dim))

    one_side = jax.random.permutation(own_key, shards_of)[block_of(target)]
    other_side = (block_of(target) + shards_of // 2) % shards_of
    return jnp.where((block_of(source) == one_side) | (block_of(source) == other_side), factor * result, result)


def steps_of(rng, dims, shards, low, high):
    factor_of, own = 1.0, jax.random.fold_in(rng, 6)
    for dim, blocks in shards:
        steps = jnp.exp(jax.random.uniform(jax.random.fold_in(own, dim), (blocks,), jnp.float32, low / len(shards), high / len(shards)))
        factor_of = factor_of * jnp.repeat(steps, dims[dim] // blocks).reshape([-1 if axis == dim else 1 for axis in range(len(dims))])
    return factor_of


def normal_values(rng, dims, scale, limit, split=(), kind=jnp.bfloat16):
    drawn = jax.random.normal(rng, dims, jnp.float32) * scale
    if len(split) > 0:
        drawn = steps_of(rng, dims, split, -0.22, 0.18) * drawn
    return jnp.clip(drawn, min=-limit, max=limit).astype(kind)


def heavy_noise(rng, shape, spread, most, split, heavy, held_as=jnp.bfloat16):
    values = spread * jax.random.normal(rng, shape, jnp.float32)
    if split:
        values = values * steps_of(rng, shape, split, -0.22, 0.18)
    return jnp.clip(strengthened(values, jax.random.fold_in(rng, 3), *heavy), -most, most).astype(held_as)


def setup_inputs(seed: int = 0) -> dict:
    splits = jax.random.split(jax.random.key(seed), 4)
    deltas = heavy_noise(splits[0], (R, PROJ, D, FF), 0.5, 3.0, ((0, 4), (2, 64)), (0, 2, 4, 2.0))
    master = normal_values(splits[1], (PROJ, D, FF), 0.5, 3.0, ((1, 4), (2, 64)), jnp.float32)
    momentum = normal_values(splits[2], (PROJ, D, FF), 0.3, 2.0, ((1, 4), (2, 64)), jnp.float32)
    return {"deltas": deltas, "master": master, "momentum": momentum}


def reference(deltas, master, momentum):
    outer = jnp.sum(deltas.astype(jnp.float32), axis=0) / deltas.shape[0]
    velocity = 0.9 * momentum + outer
    updated = master - 0.7 * (outer + 0.9 * velocity)
    return updated, velocity, updated.astype(jnp.bfloat16)
```

```python
import jax
import jax.numpy as jnp
import numpy as np
from jax import lax
from jax.experimental import pallas as pl
from jax.experimental.pallas import tpu as pltpu
from jax.sharding import Mesh
from jax.sharding import PartitionSpec as P

AXES = ("xh", "c", "zh", "zm", "z0", "y", "xl")
SIZES = (2, 2, 2, 2, 2, 4, 2)
PLANE = ("zh", "zm", "z0", "y")
REPLICA = ("xh", "c")
FSDP = ("zh", "zm", "z0", "y", "xl")


def pairs(flip):
    grid = np.arange(np.prod(SIZES)).reshape(SIZES)
    moved = np.flip(grid, [AXES.index(name) for name in flip])
    return [(int(s), int(t)) for s, t in zip(grid.ravel(), moved.ravel(), strict=True)]


def swap(value, *flip):
    return lax.ppermute(value, AXES, pairs(flip))


VMEM = pl.BlockSpec(memory_space=pltpu.VMEM)
SMEM = pl.BlockSpec(memory_space=pltpu.SMEM)


def first_sum(where, mine, theirs):
    rows, width = mine.shape[1], 256
    blocks = mine.shape[2] // (2 * width)

    def kernel(where_ref, mine_ref, theirs_ref, keep_ref, send_ref):
        kept = where_ref[1]

        def part(k, side):
            at = pl.ds(pl.multiple_of(k * 2 * width + side * width, width), width)
            return mine_ref[0, :, at].astype(jnp.float32) + theirs_ref[:, at].astype(jnp.float32)

        def body(k, carry):
            keep_ref[k] = part(k, kept)
            send_ref[k] = part(k, 1 - kept).astype(jnp.bfloat16)
            return carry

        lax.fori_loop(0, blocks, body, 0, unroll=4)

    return pl.pallas_call(
        kernel,
        grid_spec=pltpu.PrefetchScalarGridSpec(
            num_scalar_prefetch=1,
            grid=(1,),
            in_specs=[pl.BlockSpec((1, rows, mine.shape[2]), lambda i, w: (w[0], 0, 0)), VMEM],
            out_specs=[VMEM, VMEM],
        ),
        out_shape=[
            jax.ShapeDtypeStruct((blocks, rows, width), jnp.float32),
            jax.ShapeDtypeStruct((blocks, rows, width), jnp.bfloat16),
        ],
        name="first_sum",
    )(where, mine, theirs)


def update(where, pieces, master, momentum):
    count, rows, width = pieces[0][0].shape

    def kernel(where_ref, p00, p01, p10, p11, m_ref, v_ref, mo_ref, vo_ref, q00, q01, q10, q11):
        c, xl = where_ref[0], where_ref[1]
        for p, s, src, dst in ((0, 0, p00, q00), (0, 1, p01, q01), (1, 0, p10, q10), (1, 1, p11, q11)):
            proj, side = jnp.bitwise_xor(c, p), jnp.bitwise_xor(xl, s)

            def body(k, carry, src=src, dst=dst, proj=proj, side=side):
                at = pl.ds(pl.multiple_of(k * 2 * rows + side * rows, rows), rows)
                outer = src[k].astype(jnp.float32) * 0.25
                velocity = 0.9 * v_ref[proj, at, :] + outer
                updated = m_ref[proj, at, :] - 0.7 * (outer + 0.9 * velocity)
                vo_ref[proj, at, :] = velocity
                mo_ref[proj, at, :] = updated
                dst[k] = updated.astype(jnp.bfloat16)
                return carry

            lax.fori_loop(0, count, body, 0, unroll=2)

    piece = jax.ShapeDtypeStruct((count, rows, width), jnp.bfloat16)
    whole = jax.ShapeDtypeStruct(master.shape, jnp.float32)
    return pl.pallas_call(
        kernel,
        in_specs=[SMEM] + [VMEM] * 6,
        out_specs=[VMEM] * 6,
        out_shape=[whole, whole, piece, piece, piece, piece],
        name="update",
    )(where, pieces[0][0], pieces[0][1], pieces[1][0], pieces[1][1], master, momentum)


def assemble(where, pieces):
    blocks, rows, width = pieces[0][0].shape

    def kernel(where_ref, p00, p01, p10, p11, out_ref):
        c, kept = where_ref[0], where_ref[1]
        for p, s, src in ((0, 0, p00), (0, 1, p01), (1, 0, p10), (1, 1, p11)):
            proj, side = jnp.bitwise_xor(c, p), jnp.bitwise_xor(kept, s)

            def body(k, carry, src=src, proj=proj, side=side):
                at = pl.ds(pl.multiple_of(k * 2 * width + side * width, width), width)
                out_ref[proj, :, at] = src[k]
                return carry

            lax.fori_loop(0, blocks, body, 0, unroll=4)

    return pl.pallas_call(
        kernel,
        in_specs=[SMEM] + [VMEM] * 4,
        out_specs=VMEM,
        out_shape=jax.ShapeDtypeStruct((2, rows, 2 * blocks * width), jnp.bfloat16),
        name="assemble",
    )(where, pieces[0][0], pieces[0][1], pieces[1][0], pieces[1][1])


def take(value, index):
    return lax.dynamic_index_in_dim(value, index, 0, keepdims=False)


def on_device(deltas, master, momentum):
    local = deltas[0]
    xh, c, zh, xl = (lax.axis_index(name) for name in ("xh", "c", "zh", "xl"))
    kept = xl ^ xh ^ zh
    sides = jnp.stack([c, kept]).astype(jnp.int32)

    theirs = swap(take(local, 1 - c), "c")
    keep, send = first_sum(sides, local, theirs)
    summed = (keep + swap(send, "xh").astype(jnp.float32)).astype(jnp.bfloat16)

    spread = lax.all_to_all(summed, PLANE, split_axis=0, concat_axis=0, tiled=True)
    spread = spread.reshape(2, 2, 8, *spread.shape[1:])
    stay, cross = take(spread, xh), take(spread, 1 - xh)
    crossed = swap(cross, "xh", "xl")
    pieces = [
        [take(stay, c), take(crossed, c)],
        [swap(take(stay, 1 - c), "c"), swap(take(crossed, 1 - c), "c")],
    ]
    updated, velocity, q00, q01, q10, q11 = update(jnp.stack([c, xl]).astype(jnp.int32), pieces, master, momentum)

    def both(mine, other):
        return jnp.where(c == 0, jnp.stack([mine, other]), jnp.stack([other, mine]))

    stay = both(q00, swap(q10, "c"))
    crossed = swap(both(q01, swap(q11, "c")), "xh", "xl")
    joined = jnp.where(xh == 0, jnp.stack([stay, crossed]), jnp.stack([crossed, stay]))
    columns = lax.all_to_all(joined.reshape(summed.shape), PLANE, split_axis=0, concat_axis=0, tiled=True)
    others = swap(columns, "xh")
    spread_out = assemble(sides, [[columns, others], [swap(columns, "c"), swap(others, "c")]])
    return updated, velocity, spread_out


def solution(mesh):
    parts = Mesh(mesh.devices.reshape(SIZES), AXES)
    return jax.shard_map(
        on_device,
        mesh=parts,
        in_specs=(P(REPLICA, None, FSDP, None), P(None, REPLICA, FSDP), P(None, REPLICA, FSDP)),
        out_specs=(P(None, REPLICA, FSDP), P(None, REPLICA, FSDP), P(None, FSDP, None)),
        check_vma=False,
    )
```

```python
import jax
import jax.numpy as jnp
import numpy as np
from jax import lax
from jax.experimental import pallas as pl
from jax.experimental.pallas import tpu as pltpu
from jax.sharding import Mesh
from jax.sharding import PartitionSpec as P

AXES = ("xh", "c", "zh", "zm", "z0", "y", "xl")
SIZES = (2, 2, 2, 2, 2, 4, 2)
PLANE = ("zh", "zm", "z0", "y")
REPLICA = ("xh", "c")
FSDP = ("zh", "zm", "z0", "y", "xl")
WIDTH = 256
GRANT = 8 << 20


NEAR = pl.BlockSpec(memory_space=pltpu.VMEM)
FAR = pl.BlockSpec(memory_space=pltpu.HBM)


def index(*names):
    total = lax.axis_index(names[0])
    for name in names[1:]:
        total = jnp.bitwise_xor(total, lax.axis_index(name))
    return total


def kept_side():
    return index("xl", "xh", "zh")


def pairs(flip):
    grid = np.arange(np.prod(SIZES)).reshape(SIZES)
    moved = np.flip(grid, [AXES.index(name) for name in flip])
    return [(int(s), int(t)) for s, t in zip(grid.ravel(), moved.ravel(), strict=True)]


def swap(value, *flip):
    return lax.ppermute(value, AXES, pairs(flip))


def on_chip(kernel, name, operands, outs, far=(), scratch=(), far_outs=(), aliases=None, to_hbm=False):
    ins = [x if k in far else pltpu.with_memory_space_constraint(x, pltpu.VMEM) for k, x in enumerate(operands)]
    return pl.pallas_call(
        kernel,
        in_specs=[FAR if k in far else NEAR for k in range(len(ins))],
        out_specs=[FAR if k in far_outs else NEAR for k in range(len(outs))],
        out_shape=[
            jax.ShapeDtypeStruct(*out) if to_hbm or k in far_outs else pltpu.VMEM(*out) for k, out in enumerate(outs)
        ],
        scratch_shapes=list(scratch),
        input_output_aliases=aliases or {},
        compiler_params=pltpu.CompilerParams(vmem_limit_bytes=GRANT),
        name=name,
    )(*ins)


def columns_of(ref, proj, k, side):
    return ref.at[proj, :, pl.ds(pl.multiple_of((2 * k + side) * WIDTH, WIDTH), WIDTH)]


def fetch(deltas, other_core):
    _, rows, columns = deltas.shape
    blocks = columns // (2 * WIDTH)

    def kernel(src, send, keep, sems):
        proj = index("c") if not other_core else 1 - index("c")
        kept = kept_side()

        def start(k, carry):
            pltpu.make_async_copy(columns_of(src, proj, k, 1 - kept), send.at[k], sems.at[0]).start()
            return carry

        def start_kept(k, carry):
            pltpu.make_async_copy(columns_of(src, proj, k, kept), keep.at[k], sems.at[1]).start()
            return carry

        lax.fori_loop(0, blocks, start, 0, unroll=4)
        lax.fori_loop(0, blocks, start_kept, 0, unroll=4)
        pltpu.make_async_copy(send, send, sems.at[0]).wait()
        pltpu.make_async_copy(keep, keep, sems.at[1]).wait()

    out = ((blocks, rows, WIDTH), deltas.dtype)
    name = "fetch_other" if other_core else "fetch_own"
    return on_chip(kernel, name, [deltas], [out, out], far=(0,), scratch=[pltpu.SemaphoreType.DMA((2,))])


def add(name, *values):
    def kernel(*refs):
        *ins, out = refs

        def body(k, carry):
            total = ins[0][k].astype(jnp.float32)
            for ref in ins[1:]:
                total += ref[k].astype(jnp.float32)
            out[k] = total.astype(out.dtype)
            return carry

        lax.fori_loop(0, out.shape[0], body, 0, unroll=4)

    return on_chip(kernel, name, values, [(values[0].shape, values[0].dtype)])[0]


def part_rows(spread):
    def kernel(src, over, across, beside):
        xh, c = index("xh"), index("c")
        over[...] = src[1 - xh, c]
        across[...] = src[1 - xh, 1 - c]
        beside[...] = src[xh, 1 - c]

    out = (spread.shape[2:], spread.dtype)
    return on_chip(kernel, "part_rows", [spread], [out, out, out])


def update(spread, over, across, beside, master, momentum):
    count, rows, _ = over.shape

    def kernel(spread_ref, over_ref, across_ref, beside_ref, m_ref, v_ref, mo_ref, vo_ref, *outs):
        xh, c, xl = index("xh"), index("c"), index("xl")
        for p, s, src in ((0, 0, spread_ref.at[xh, c]), (0, 1, over_ref), (1, 0, beside_ref), (1, 1, across_ref)):
            proj, side, dst = jnp.bitwise_xor(c, p), jnp.bitwise_xor(xl, s), outs[2 * p + s]

            def body(k, carry, src=src, dst=dst, proj=proj, side=side):
                at = pl.ds(pl.multiple_of((2 * k + side) * rows, rows), rows)
                outer = src[k].astype(jnp.float32) * 0.25
                velocity = 0.9 * v_ref[proj, at, :] + outer
                updated = m_ref[proj, at, :] - 0.7 * (outer + 0.9 * velocity)
                vo_ref[proj, at, :] = velocity
                mo_ref[proj, at, :] = updated
                dst[k] = updated.astype(dst.dtype)
                return carry

            lax.fori_loop(0, count, body, 0, unroll=2)

    whole, piece = (master.shape, master.dtype), (over.shape, over.dtype)
    operands = [spread, over, across, beside, master, momentum]
    return on_chip(kernel, "update", operands, [whole, whole, piece, piece, piece, piece])


def store(first, second):
    def kernel(first_ref, second_ref, first_out, second_out, sems):
        copies = [
            pltpu.make_async_copy(first_ref, first_out, sems.at[0]),
            pltpu.make_async_copy(second_ref, second_out, sems.at[1]),
        ]
        for copy in copies:
            copy.start()
        for copy in copies:
            copy.wait()

    out = (first.shape, first.dtype)
    return on_chip(
        kernel, "store", [first, second], [out, out], far_outs=(0, 1), scratch=[pltpu.SemaphoreType.DMA((2,))]
    )


def join_rows(own, over, across, beside):
    def kernel(own_ref, over_ref, across_ref, beside_ref, out):
        xh, c = index("xh"), index("c")
        out[xh, c] = own_ref[...]
        out[1 - xh, c] = over_ref[...]
        out[1 - xh, 1 - c] = across_ref[...]
        out[xh, 1 - c] = beside_ref[...]

    return on_chip(kernel, "join_rows", [own, over, across, beside], [((2, 2, *own.shape), own.dtype)])[0]


def place(own, other, kept, into=None):
    blocks, rows, _ = own.shape

    def kernel(*refs):
        own_ref, other_ref, out, sems = refs[0], refs[1], refs[-2], refs[-1]
        c, side = index("c"), kept_side() if kept else 1 - kept_side()
        for p, src in ((0, own_ref), (1, other_ref)):

            def start(k, carry, src=src, p=p):
                target = columns_of(out, jnp.bitwise_xor(c, p), k, side)
                pltpu.make_async_copy(src.at[k], target, sems.at[p]).start()
                return carry

            lax.fori_loop(0, blocks, start, 0, unroll=4)
        for p, src in ((0, own_ref), (1, other_ref)):
            pltpu.make_async_copy(src, src, sems.at[p]).wait()

    operands = [own, other] + ([] if into is None else [into])
    return on_chip(
        kernel,
        "place_kept" if kept else "place_rest",
        operands,
        [((2, rows, 2 * blocks * WIDTH), own.dtype)],
        far=(2,),
        far_outs=(0,),
        scratch=[pltpu.SemaphoreType.DMA((2,))],
        aliases=None if into is None else {2: 0},
    )[0]


def on_device(deltas, master, momentum):
    local = deltas[0]

    send_other, keep_other = fetch(local, True)
    theirs_send = swap(send_other, "c")
    theirs_keep = swap(keep_other, "c")
    mine_send, mine_keep = fetch(local, False)
    across_x = swap(add("sum_sent", mine_send, theirs_send), "xh")
    summed = add("sum_kept", mine_keep, theirs_keep, across_x)

    spread = lax.all_to_all(summed, PLANE, split_axis=0, concat_axis=0, tiled=True)
    spread = spread.reshape(2, 2, -1, *spread.shape[1:])
    over, across, beside = part_rows(spread)
    over, across, beside = swap(over, "xh", "xl"), swap(across, "xh", "xl", "c"), swap(beside, "c")
    updated, velocity, own, over, beside, across = update(spread, over, across, beside, master, momentum)
    updated, velocity = store(updated, velocity)

    over, across, beside = swap(over, "xh", "xl"), swap(across, "xh", "xl", "c"), swap(beside, "c")
    joined = join_rows(own, over, across, beside).reshape(summed.shape)
    kept = lax.all_to_all(joined, PLANE, split_axis=0, concat_axis=0, tiled=True)
    rest = swap(kept, "xh")
    first = place(kept, swap(kept, "c"), True)
    rest, first, updated, velocity = lax.optimization_barrier((rest, first, updated, velocity))
    return updated, velocity, place(rest, swap(rest, "c"), False, first)


def solution(mesh):
    parts = Mesh(mesh.devices.reshape(SIZES), AXES)
    return jax.shard_map(
        on_device,
        mesh=parts,
        in_specs=(P(REPLICA, None, FSDP, None), P(None, REPLICA, FSDP), P(None, REPLICA, FSDP)),
        out_specs=(P(None, REPLICA, FSDP), P(None, REPLICA, FSDP), P(None, FSDP, None)),
        check_vma=False,
    )
```

```python
import jax
import jax.numpy as jnp
import numpy as np
from jax import lax
from jax.experimental import pallas as pl
from jax.experimental.pallas import tpu as pltpu
from jax.sharding import Mesh
from jax.sharding import PartitionSpec as P


AXES = ("xh", "c", "zh", "zm", "z0", "y", "xl")
SIZES = (2, 2, 2, 2, 2, 4, 2)
PLANE = ("zh", "zm", "z0", "y")
REPLICA = ("xh", "c")
FSDP = ("zh", "zm", "z0", "y", "xl")
WIDTH = 256
HALVES = 2
GRANT = 8 << 20


NEAR = pl.BlockSpec(memory_space=pltpu.VMEM)
FAR = pl.BlockSpec(memory_space=pltpu.HBM)


def index(*names):
    total = lax.axis_index(names[0])
    for name in names[1:]:
        total = jnp.bitwise_xor(total, lax.axis_index(name))
    return total


def kept_side():
    return index("xl", "xh", "zh")


def pairs(flip):
    grid = np.arange(np.prod(SIZES)).reshape(SIZES)
    moved = np.flip(grid, [AXES.index(name) for name in flip])
    return [(int(s), int(t)) for s, t in zip(grid.ravel(), moved.ravel(), strict=True)]


def swap(value, *flip):
    return lax.ppermute(value, AXES, pairs(flip))


def exchange(value):
    return lax.all_to_all(value, PLANE, split_axis=0, concat_axis=0, tiled=True)


def on_chip(kernel, operands, outs, far=(), scratch=(), far_outs=(), aliases=None):
    ins = [
        pltpu.with_memory_space_constraint(x, pltpu.HBM if k in far else pltpu.VMEM) for k, x in enumerate(operands)
    ]
    return pl.pallas_call(
        kernel,
        in_specs=[FAR if k in far else NEAR for k in range(len(ins))],
        out_specs=[FAR if k in far_outs else NEAR for k in range(len(outs))],
        out_shape=[
            jax.ShapeDtypeStruct(*out) if k in far_outs else pltpu.VMEM(*out) for k, out in enumerate(outs)
        ],
        scratch_shapes=list(scratch),
        input_output_aliases=aliases or {},
        compiler_params=pltpu.CompilerParams(vmem_limit_bytes=GRANT),
    )(*ins)


def block_of(ref, proj, half, rows, k, side):
    at = pl.ds(pl.multiple_of((2 * k + side) * WIDTH, WIDTH), WIDTH)
    return ref.at[proj, pl.ds(half * rows, rows), at]


def fetch(deltas, halves, other_core):
    rows, blocks = deltas.shape[1] // HALVES, deltas.shape[2] // (2 * WIDTH)

    def kernel(src, *refs):
        outs, sems = refs[:-1], refs[-1]
        proj = index("c") if not other_core else 1 - index("c")
        kept = kept_side()
        for j, (half, out) in enumerate(zip(halves, outs, strict=True)):

            def start(k, carry, j=j, half=half, out=out):
                for s, side in enumerate((1 - kept, kept)):
                    pltpu.make_async_copy(block_of(src, proj, half, rows, k, side), out.at[s, k], sems.at[j]).start()
                return carry

            lax.fori_loop(0, blocks, start, 0, unroll=4)
        for j, out in enumerate(outs):
            pltpu.make_async_copy(out, out, sems.at[j]).wait()

    shapes = [((2, blocks, rows, WIDTH), deltas.dtype)] * len(halves)
    return on_chip(kernel, [deltas], shapes, far=(0,), scratch=[pltpu.SemaphoreType.DMA((len(halves),))])


def add(side, *values):
    shape = values[0].shape[-3:]

    def kernel(*refs):
        *ins, out = refs

        def body(k, carry):
            parts = [ref[side, k] if len(ref.shape) == 4 else ref[k] for ref in ins]
            total = parts[0].astype(jnp.float32)
            for part in parts[1:]:
                total += part.astype(jnp.float32)
            out[k] = total.astype(out.dtype)
            return carry

        lax.fori_loop(0, out.shape[0], body, 0, unroll=4)

    return on_chip(kernel, values, [(shape, values[0].dtype)])[0]


def part_rows(spread):
    def kernel(src, over, across, beside):
        xh, c = index("xh"), index("c")
        over[...] = src[1 - xh, c]
        across[...] = src[1 - xh, 1 - c]
        beside[...] = src[xh, 1 - c]

    out = (spread.shape[2:], spread.dtype)
    return on_chip(kernel, [spread], [out, out, out])


def update(half, spread, over, across, beside, master, momentum, into):
    count, rows, _ = over.shape
    blocks = 2 * count

    def kernel(spread_ref, over_ref, across_ref, beside_ref, m_far, v_far, *refs):
        mo_far, vo_far, q00, q01, q10, q11, m_ref, v_ref, sems = refs[-9:]
        xh, c, xl = index("xh"), index("c"), index("xl")

        def copies(work):
            def each(k, carry):
                at = pl.ds(pl.multiple_of(k * HALVES * rows + half * rows, rows), rows)
                for proj in range(2):
                    work(proj, k, at)
                return carry

            lax.fori_loop(0, blocks, each, 0, unroll=2)

        def read(proj, k, at):
            pltpu.make_async_copy(m_far.at[proj, at, :], m_ref.at[proj, k], sems.at[0]).start()
            pltpu.make_async_copy(v_far.at[proj, at, :], v_ref.at[proj, k], sems.at[1]).start()

        def write(proj, k, at):
            pltpu.make_async_copy(m_ref.at[proj, k], mo_far.at[proj, at, :], sems.at[0]).start()
            pltpu.make_async_copy(v_ref.at[proj, k], vo_far.at[proj, at, :], sems.at[1]).start()

        def wait():
            pltpu.make_async_copy(m_ref, m_ref, sems.at[0]).wait()
            pltpu.make_async_copy(v_ref, v_ref, sems.at[1]).wait()

        copies(read)
        wait()
        for p, s, src, dst in (
            (0, 0, spread_ref.at[xh, c], q00),
            (0, 1, over_ref, q01),
            (1, 0, beside_ref, q10),
            (1, 1, across_ref, q11),
        ):
            proj, side = jnp.bitwise_xor(c, p), jnp.bitwise_xor(xl, s)

            def body(k, carry, src=src, dst=dst, proj=proj, side=side):
                block = 2 * k + side
                outer = src[k].astype(jnp.float32) * 0.25
                velocity = 0.9 * v_ref[proj, block] + outer
                updated = m_ref[proj, block] - 0.7 * (outer + 0.9 * velocity)
                v_ref[proj, block] = velocity
                m_ref[proj, block] = updated
                dst[k] = updated.astype(dst.dtype)
                return carry

            lax.fori_loop(0, count, body, 0, unroll=2)
        copies(write)
        wait()

    whole, piece = (master.shape, master.dtype), (over.shape, over.dtype)
    operands = [spread, over, across, beside, master, momentum, *into]
    held = pltpu.VMEM((2, blocks, rows, WIDTH), master.dtype)
    return on_chip(
        kernel,
        operands,
        [whole, whole, piece, piece, piece, piece],
        far=(4, 5, 6, 7),
        far_outs=(0, 1),
        scratch=[held, held, pltpu.SemaphoreType.DMA((2,))],
        aliases={6: 0, 7: 1} if into else None,
    )


def join_rows(own, over, across, beside):
    def kernel(own_ref, over_ref, across_ref, beside_ref, out):
        xh, c = index("xh"), index("c")
        out[xh, c] = own_ref[...]
        out[1 - xh, c] = over_ref[...]
        out[1 - xh, 1 - c] = across_ref[...]
        out[xh, 1 - c] = beside_ref[...]

    return on_chip(kernel, [own, over, across, beside], [((2, 2, *own.shape), own.dtype)])[0]


def place(half, pieces, into=None):
    blocks, rows, _ = pieces[0][0].shape
    count = len(pieces)

    def kernel(*refs):
        ins, out, sems = refs[:count], refs[-2], refs[-1]
        for j, (src, (_, other, kept)) in enumerate(zip(ins, pieces, strict=True)):
            proj = 1 - index("c") if other else index("c")
            side = kept_side() if kept else 1 - kept_side()

            def start(k, carry, j=j, src=src, proj=proj, side=side):
                pltpu.make_async_copy(src.at[k], block_of(out, proj, half, rows, k, side), sems.at[j]).start()
                return carry

            lax.fori_loop(0, blocks, start, 0, unroll=4)
        for j, src in enumerate(ins):
            pltpu.make_async_copy(src, src, sems.at[j]).wait()

    operands = [piece[0] for piece in pieces] + ([] if into is None else [into])
    return on_chip(
        kernel,
        operands,
        [((2, HALVES * rows, 2 * blocks * WIDTH), operands[0].dtype)],
        far=(count,),
        far_outs=(0,),
        scratch=[pltpu.SemaphoreType.DMA((count,))],
        aliases=None if into is None else {count: 0},
    )[0]


def on_device(deltas, master, momentum):
    return step(deltas[0], master, momentum)


def across_rows(over, across, beside):
    return swap(over, "xh", "xl"), swap(across, "xh", "xl", "c"), swap(beside, "c")


def across_x(value):
    return swap(value, "xh")


def step(local, master, momentum):
    both = range(HALVES)

    theirs = [swap(fetch(local, [h], True)[0], "c") for h in both]
    mine = fetch(local, list(both), False)
    summed = [add(1, mine[h], theirs[h], across_x(add(0, mine[h], theirs[h]))) for h in both]

    state, joined = (), []
    for h in both:
        spread = exchange(summed[h])
        spread = spread.reshape(2, 2, -1, *spread.shape[1:])
        moved = across_rows(*part_rows(spread))
        *state, own, over, beside, across = update(h, spread, *moved, master, momentum, state)
        moved = across_rows(over, across, beside)
        joined.append(join_rows(own, *moved).reshape(summed[h].shape))

    params = None
    for h in both:
        kept = exchange(joined[h])
        rest = across_x(kept)
        pieces = [(kept, False, True), (swap(kept, "c"), True, True)]
        if h == HALVES - 1:
            params = place(h, pieces, params)
            pieces = []
            rest, params = lax.optimization_barrier((rest, params))
        params = place(h, [*pieces, (rest, False, False), (swap(rest, "c"), True, False)], params)
    return *state, params


def solution(mesh):
    parts = Mesh(mesh.devices.reshape(SIZES), AXES)
    return jax.shard_map(
        on_device,
        mesh=parts,
        in_specs=(P(REPLICA, None, FSDP, None), P(None, REPLICA, FSDP), P(None, REPLICA, FSDP)),
        out_specs=(P(None, REPLICA, FSDP), P(None, REPLICA, FSDP), P(None, FSDP, None)),
        check_vma=False,
    )
```

```python
import jax
import jax.numpy as jnp
import numpy as np
from jax import lax
from jax.experimental import pallas as pl
from jax.experimental.pallas import tpu as pltpu
from jax.sharding import Mesh
from jax.sharding import PartitionSpec as P


AXES = ("xh", "c", "zh", "zm", "z0", "y", "xl")
SIZES = (2, 2, 2, 2, 2, 4, 2)
PLANE = ("zh", "zm", "z0", "y")
REPLICA = ("xh", "c")
FSDP = ("zh", "zm", "z0", "y", "xl")
WIDTH = 256
COLUMNS = 64 * WIDTH
CUT_IN, CUT_OUT = 12, 24
GRANT = 8 << 20


NEAR = pl.BlockSpec(memory_space=pltpu.VMEM)
FAR = pl.BlockSpec(memory_space=pltpu.HBM)


def index(*names):
    total = lax.axis_index(names[0])
    for name in names[1:]:
        total = jnp.bitwise_xor(total, lax.axis_index(name))
    return total


def kept_side():
    return index("xl", "xh", "zh")


def pairs(flip):
    grid = np.arange(np.prod(SIZES)).reshape(SIZES)
    moved = np.flip(grid, [AXES.index(name) for name in flip])
    return [(int(s), int(t)) for s, t in zip(grid.ravel(), moved.ravel(), strict=True)]


def swap(value, *flip):
    return lax.ppermute(value, AXES, pairs(flip))


def exchange(value):
    return lax.all_to_all(value, PLANE, split_axis=0, concat_axis=0, tiled=True)


def on_chip(kernel, operands, outs, far=(), scratch=(), far_outs=(), aliases=None):
    ins = [
        pltpu.with_memory_space_constraint(x, pltpu.HBM if k in far else pltpu.VMEM) for k, x in enumerate(operands)
    ]
    return pl.pallas_call(
        kernel,
        in_specs=[FAR if k in far else NEAR for k in range(len(ins))],
        out_specs=[FAR if k in far_outs else NEAR for k in range(len(outs))],
        out_shape=[
            jax.ShapeDtypeStruct(*out) if k in far_outs else pltpu.VMEM(*out) for k, out in enumerate(outs)
        ],
        scratch_shapes=list(scratch),
        input_output_aliases=aliases or {},
        compiler_params=pltpu.CompilerParams(vmem_limit_bytes=GRANT),
    )(*ins)


def columns_of(ref, proj, k, side):
    return ref.at[proj, :, pl.ds(pl.multiple_of((2 * k + side) * WIDTH, WIDTH), WIDTH)]


def fetch(deltas, other_core, kept, first, count):
    def kernel(src, out, sem):
        proj = 1 - index("c") if other_core else index("c")
        side = kept_side() if kept else 1 - kept_side()

        def start(k, carry):
            pltpu.make_async_copy(columns_of(src, proj, first + k, side), out.at[k], sem).start()
            return carry

        lax.fori_loop(0, count, start, 0, unroll=4)
        pltpu.make_async_copy(out, out, sem).wait()

    out = ((count, deltas.shape[1], WIDTH), deltas.dtype)
    return on_chip(kernel, [deltas], [out], far=(0,), scratch=[pltpu.SemaphoreType.DMA])[0]


def add(*values):
    def kernel(*refs):
        *ins, out = refs

        def body(k, carry):
            total = ins[0][k].astype(jnp.float32)
            for ref in ins[1:]:
                total += ref[k].astype(jnp.float32)
            out[k] = total.astype(out.dtype)
            return carry

        lax.fori_loop(0, out.shape[0], body, 0, unroll=4)

    return on_chip(kernel, values, [(values[0].shape, values[0].dtype)])[0]


def add_kept(mine, theirs, sent):
    def kernel(mine_ref, theirs_ref, *refs):
        *parts, out = refs
        first = 0
        for part in parts:

            def body(k, carry, part=part, first=first):
                total = mine_ref[first + k].astype(jnp.float32) + theirs_ref[first + k].astype(jnp.float32)
                out[first + k] = (total + part[k].astype(jnp.float32)).astype(out.dtype)
                return carry

            lax.fori_loop(0, part.shape[0], body, 0, unroll=4)
            first += part.shape[0]

    return on_chip(kernel, [mine, theirs, *sent], [(mine.shape, mine.dtype)])[0]


def part_rows(spread):
    def kernel(src, over, across, beside):
        xh, c = index("xh"), index("c")
        over[...] = src[1 - xh, c]
        across[...] = src[1 - xh, 1 - c]
        beside[...] = src[xh, 1 - c]

    out = (spread.shape[2:], spread.dtype)
    return on_chip(kernel, [spread], [out, out, out])


def update(spread, over, across, beside, master, momentum):
    count, rows, _ = over.shape

    def kernel(spread_ref, over_ref, across_ref, beside_ref, m_ref, v_ref, mo_ref, vo_ref, *outs):
        xh, c, xl = index("xh"), index("c"), index("xl")
        for p, s, src in ((0, 0, spread_ref.at[xh, c]), (0, 1, over_ref), (1, 0, beside_ref), (1, 1, across_ref)):
            proj, side, dst = jnp.bitwise_xor(c, p), jnp.bitwise_xor(xl, s), outs[2 * p + s]

            def body(k, carry, src=src, dst=dst, proj=proj, side=side):
                at = pl.ds(pl.multiple_of((2 * k + side) * rows, rows), rows)
                outer = src[k].astype(jnp.float32) * 0.25
                velocity = 0.9 * v_ref[proj, at, :] + outer
                updated = m_ref[proj, at, :] - 0.7 * (outer + 0.9 * velocity)
                vo_ref[proj, at, :] = velocity
                mo_ref[proj, at, :] = updated
                dst[k] = updated.astype(dst.dtype)
                return carry

            lax.fori_loop(0, count, body, 0, unroll=2)

    whole, piece = (master.shape, master.dtype), (over.shape, over.dtype)
    operands = [spread, over, across, beside, master, momentum]
    return on_chip(kernel, operands, [whole, whole, piece, piece, piece, piece])


def store(first, second):
    def kernel(first_ref, second_ref, first_out, second_out, sems):
        copies = [
            pltpu.make_async_copy(first_ref, first_out, sems.at[0]),
            pltpu.make_async_copy(second_ref, second_out, sems.at[1]),
        ]
        for copy in copies:
            copy.start()
        for copy in copies:
            copy.wait()

    out = (first.shape, first.dtype)
    return on_chip(kernel, [first, second], [out, out], far_outs=(0, 1), scratch=[pltpu.SemaphoreType.DMA((2,))])


def join_rows(own, over, across, beside):
    def kernel(own_ref, over_ref, across_ref, beside_ref, out):
        xh, c = index("xh"), index("c")
        out[xh, c] = own_ref[...]
        out[1 - xh, c] = over_ref[...]
        out[1 - xh, 1 - c] = across_ref[...]
        out[xh, 1 - c] = beside_ref[...]

    return on_chip(kernel, [own, over, across, beside], [((2, 2, *own.shape), own.dtype)])[0]


def place(pieces, into=None):
    rows = pieces[0][0].shape[1]
    count = len(pieces)

    def kernel(*refs):
        ins, out, sems = refs[:count], refs[-2], refs[-1]
        for j, (src, (_, first, other, kept)) in enumerate(zip(ins, pieces, strict=True)):
            proj = 1 - index("c") if other else index("c")
            side = kept_side() if kept else 1 - kept_side()

            def start(k, carry, j=j, src=src, first=first, proj=proj, side=side):
                pltpu.make_async_copy(src.at[k], columns_of(out, proj, first + k, side), sems.at[j]).start()
                return carry

            lax.fori_loop(0, src.shape[0], start, 0, unroll=4)
        for j, src in enumerate(ins):
            pltpu.make_async_copy(src, src, sems.at[j]).wait()

    operands = [piece[0] for piece in pieces] + ([] if into is None else [into])
    return on_chip(
        kernel,
        operands,
        [((2, rows, COLUMNS), operands[0].dtype)],
        far=(count,),
        far_outs=(0,),
        scratch=[pltpu.SemaphoreType.DMA((count,))],
        aliases=None if into is None else {count: 0},
    )[0]


def on_device(deltas, master, momentum):
    return step(deltas[0], master, momentum)


def across_rows(over, across, beside):
    return swap(over, "xh", "xl"), swap(across, "xh", "xl", "c"), swap(beside, "c")


def step(local, master, momentum):
    blocks = local.shape[2] // (2 * WIDTH)
    sent = []
    for first, count in ((0, CUT_IN), (CUT_IN, blocks - CUT_IN)):
        theirs = swap(fetch(local, True, False, first, count), "c")
        sent.append(swap(add(fetch(local, False, False, first, count), theirs), "xh"))
    theirs = swap(fetch(local, True, True, 0, blocks), "c")
    mine = fetch(local, False, True, 0, blocks)
    summed = add_kept(mine, theirs, sent)

    spread = exchange(summed)
    spread = spread.reshape(2, 2, -1, *spread.shape[1:])
    moved = across_rows(*part_rows(spread))
    updated, velocity, own, over, beside, across = update(spread, *moved, master, momentum)

    moved = across_rows(over, across, beside)
    kept = exchange(join_rows(own, *moved).reshape(summed.shape))
    early, late = swap(kept[:CUT_OUT], "xh"), swap(kept[CUT_OUT:], "xh")
    pieces = [(kept, 0, False, True), (swap(kept, "c"), 0, True, True)]
    params = place(pieces)
    updated, velocity = store(updated, velocity)
    early, params, updated, velocity = lax.optimization_barrier((early, params, updated, velocity))
    params = place([(early, 0, False, False), (swap(early, "c"), 0, True, False)], params)
    params = place([(late, CUT_OUT, False, False), (swap(late, "c"), CUT_OUT, True, False)], params)
    return updated, velocity, params


def solution(mesh):
    parts = Mesh(mesh.devices.reshape(SIZES), AXES)
    return jax.shard_map(
        on_device,
        mesh=parts,
        in_specs=(P(REPLICA, None, FSDP, None), P(None, REPLICA, FSDP), P(None, REPLICA, FSDP)),
        out_specs=(P(None, REPLICA, FSDP), P(None, REPLICA, FSDP), P(None, FSDP, None)),
        check_vma=False,
    )
```

```python
import jax
import jax.numpy as jnp
import numpy as np
from jax import lax
from jax.experimental import pallas as pl
from jax.experimental.pallas import tpu as pltpu
from jax.sharding import Mesh
from jax.sharding import PartitionSpec as P


AXES = ("xh", "c", "zh", "zm", "z0", "y", "xl")
SIZES = (2, 2, 2, 2, 2, 4, 2)
PLANE = ("zh", "zm", "z0", "y")
REPLICA = ("xh", "c")
FSDP = ("zh", "zm", "z0", "y", "xl")
WIDTH = 256
COLUMNS = 64 * WIDTH
CUT = 24
GRANT = 8 << 20


NEAR = pl.BlockSpec(memory_space=pltpu.VMEM)
FAR = pl.BlockSpec(memory_space=pltpu.HBM)


def index(*names):
    total = lax.axis_index(names[0])
    for name in names[1:]:
        total = jnp.bitwise_xor(total, lax.axis_index(name))
    return total


def kept_side():
    return index("xl", "xh", "zh")


def pairs(flip):
    grid = np.arange(np.prod(SIZES)).reshape(SIZES)
    moved = np.flip(grid, [AXES.index(name) for name in flip])
    return [(int(s), int(t)) for s, t in zip(grid.ravel(), moved.ravel(), strict=True)]


def swap(value, *flip):
    return lax.ppermute(value, AXES, pairs(flip))


def exchange(value, axes):
    return lax.all_to_all(value, axes, split_axis=0, concat_axis=0, tiled=True)


def on_chip(kernel, operands, outs, far=(), scratch=(), far_outs=(), aliases=None):
    ins = [
        pltpu.with_memory_space_constraint(x, pltpu.HBM if k in far else pltpu.VMEM) for k, x in enumerate(operands)
    ]
    return pl.pallas_call(
        kernel,
        in_specs=[FAR if k in far else NEAR for k in range(len(ins))],
        out_specs=[FAR if k in far_outs else NEAR for k in range(len(outs))],
        out_shape=[
            jax.ShapeDtypeStruct(*out) if k in far_outs else pltpu.VMEM(*out) for k, out in enumerate(outs)
        ],
        scratch_shapes=list(scratch),
        input_output_aliases=aliases or {},
        compiler_params=pltpu.CompilerParams(vmem_limit_bytes=GRANT),
    )(*ins)


def columns_of(ref, proj, block):
    return ref.at[proj, :, pl.ds(pl.multiple_of(block * WIDTH, WIDTH), WIDTH)]


def fetch(deltas, other_core):
    count = deltas.shape[2] // WIDTH

    def kernel(src, out, sem):
        proj = 1 - index("c") if other_core else index("c")

        def start(k, carry):
            pltpu.make_async_copy(columns_of(src, proj, k), out.at[k], sem).start()
            return carry

        lax.fori_loop(0, count, start, 0, unroll=4)
        pltpu.make_async_copy(out, out, sem).wait()

    out = ((count, deltas.shape[1], WIDTH), deltas.dtype)
    return on_chip(kernel, [deltas], [out], far=(0,), scratch=[pltpu.SemaphoreType.DMA])[0]


def add(*values):
    def kernel(*refs):
        *ins, out = refs

        def body(k, carry):
            total = ins[0][k].astype(jnp.float32)
            for ref in ins[1:]:
                total += ref[k].astype(jnp.float32)
            out[k] = total.astype(out.dtype)
            return carry

        lax.fori_loop(0, out.shape[0], body, 0, unroll=4)

    return on_chip(kernel, values, [(values[0].shape, values[0].dtype)])[0]


def part_rows(spread):
    def kernel(src, over, beside_other, beside_own):
        xh, c = index("xh"), index("c")
        over[...] = src[1 - xh, c]
        beside_other[...] = src[1 - xh, 1 - c]
        beside_own[...] = src[xh, 1 - c]

    out = (spread.shape[2:], spread.dtype)
    return on_chip(kernel, [spread], [out, out, out])


def update(spread, over, beside, across, master, momentum):
    blocks, rows, _ = over.shape

    def kernel(spread_ref, over_ref, beside_ref, across_ref, m_ref, v_ref, mo_ref, vo_ref, *outs):
        xh, c, xl = index("xh"), index("c"), index("xl")
        for p, here, there in ((0, spread_ref.at[xh, c], over_ref), (1, beside_ref, across_ref)):
            proj = jnp.bitwise_xor(c, p)
            for s in range(2):
                side, dst = jnp.bitwise_xor(xl, s), outs[2 * p + s]

                def body(k, carry, here=here, there=there, dst=dst, proj=proj, side=side):
                    block = 2 * k + side
                    at = pl.ds(pl.multiple_of(block * rows, rows), rows)
                    outer = (here[block].astype(jnp.float32) + there[block].astype(jnp.float32)) * 0.25
                    velocity = 0.9 * v_ref[proj, at, :] + outer
                    updated = m_ref[proj, at, :] - 0.7 * (outer + 0.9 * velocity)
                    vo_ref[proj, at, :] = velocity
                    mo_ref[proj, at, :] = updated
                    dst[k] = updated.astype(dst.dtype)
                    return carry

                lax.fori_loop(0, blocks // 2, body, 0, unroll=2)

    whole, piece = (master.shape, master.dtype), ((blocks // 2, *over.shape[1:]), over.dtype)
    operands = [spread, over, beside, across, master, momentum]
    return on_chip(kernel, operands, [whole, whole, piece, piece, piece, piece])


def store(first, second):
    def kernel(first_ref, second_ref, first_out, second_out, sems):
        copies = [
            pltpu.make_async_copy(first_ref, first_out, sems.at[0]),
            pltpu.make_async_copy(second_ref, second_out, sems.at[1]),
        ]
        for copy in copies:
            copy.start()
        for copy in copies:
            copy.wait()

    out = (first.shape, first.dtype)
    return on_chip(kernel, [first, second], [out, out], far_outs=(0, 1), scratch=[pltpu.SemaphoreType.DMA((2,))])


def join_rows(own, over, across, beside):
    def kernel(own_ref, over_ref, across_ref, beside_ref, out):
        xh, c = index("xh"), index("c")
        out[xh, c] = own_ref[...]
        out[1 - xh, c] = over_ref[...]
        out[1 - xh, 1 - c] = across_ref[...]
        out[xh, 1 - c] = beside_ref[...]

    return on_chip(kernel, [own, over, across, beside], [((2, 2, *own.shape), own.dtype)])[0]


def place(pieces, into=None):
    rows = pieces[0][0].shape[1]
    count = len(pieces)

    def kernel(*refs):
        ins, out, sems = refs[:count], refs[-2], refs[-1]
        for j, (src, (_, first, other, kept)) in enumerate(zip(ins, pieces, strict=True)):
            proj = 1 - index("c") if other else index("c")
            side = kept_side() if kept else 1 - kept_side()

            def start(k, carry, j=j, src=src, first=first, proj=proj, side=side):
                pltpu.make_async_copy(src.at[k], columns_of(out, proj, 2 * (first + k) + side), sems.at[j]).start()
                return carry

            lax.fori_loop(0, src.shape[0], start, 0, unroll=4)
        for j, src in enumerate(ins):
            pltpu.make_async_copy(src, src, sems.at[j]).wait()

    operands = [piece[0] for piece in pieces] + ([] if into is None else [into])
    return on_chip(
        kernel,
        operands,
        [((2, rows, COLUMNS), operands[0].dtype)],
        far=(count,),
        far_outs=(0,),
        scratch=[pltpu.SemaphoreType.DMA((count,))],
        aliases=None if into is None else {count: 0},
    )[0]


def on_device(deltas, master, momentum):
    return step(deltas[0], master, momentum)


def across_rows(over, across, beside):
    return swap(over, "xh", "xl"), swap(across, "xh", "xl", "c"), swap(beside, "c")


def step(local, master, momentum):
    theirs = swap(fetch(local, True), "c")
    summed = add(fetch(local, False), theirs)

    spread = exchange(summed, FSDP)
    spread = spread.reshape(2, 2, -1, *spread.shape[1:])
    over, beside_other, beside_own = part_rows(spread)
    over = swap(over, "xh")
    across = swap(swap(beside_other, "c"), "xh")
    beside = swap(beside_own, "c")
    updated, velocity, own, over, beside, across = update(spread, over, beside, across, master, momentum)

    moved = across_rows(over, across, beside)
    joined = join_rows(own, *moved)
    kept = exchange(joined.reshape(-1, *joined.shape[3:]), PLANE)
    early, late = swap(kept[:CUT], "xh"), swap(kept[CUT:], "xh")
    pieces = [(kept, 0, False, True), (swap(kept, "c"), 0, True, True)]
    params = place(pieces)
    updated, velocity = store(updated, velocity)
    early, params, updated, velocity = lax.optimization_barrier((early, params, updated, velocity))
    params = place([(early, 0, False, False), (swap(early, "c"), 0, True, False)], params)
    params = place([(late, CUT, False, False), (swap(late, "c"), CUT, True, False)], params)
    return updated, velocity, params


def solution(mesh):
    parts = Mesh(mesh.devices.reshape(SIZES), AXES)
    return jax.shard_map(
        on_device,
        mesh=parts,
        in_specs=(P(REPLICA, None, FSDP, None), P(None, REPLICA, FSDP), P(None, REPLICA, FSDP)),
        out_specs=(P(None, REPLICA, FSDP), P(None, REPLICA, FSDP), P(None, FSDP, None)),
        check_vma=False,
    )
```

```python
import jax
import jax.numpy as jnp
import numpy as np
from jax import lax
from jax.experimental import pallas as pl
from jax.experimental.pallas import tpu as pltpu
from jax.sharding import Mesh
from jax.sharding import PartitionSpec as P


AXES = ("xh", "c", "zh", "zm", "z0", "y", "xl")
SIZES = (2, 2, 2, 2, 2, 4, 2)
PLANE = ("zh", "zm", "z0", "y")
REPLICA = ("xh", "c")
FSDP = ("zh", "zm", "z0", "y", "xl")
WIDTH = 256
COLUMNS = 64 * WIDTH
CUT = 24
GRANT = 8 << 20


NEAR = pl.BlockSpec(memory_space=pltpu.VMEM)
FAR = pl.BlockSpec(memory_space=pltpu.HBM)


def index(*names):
    total = lax.axis_index(names[0])
    for name in names[1:]:
        total = jnp.bitwise_xor(total, lax.axis_index(name))
    return total


def kept_side():
    return index("xl", "xh", "zh")


def pairs(flip):
    grid = np.arange(np.prod(SIZES)).reshape(SIZES)
    moved = np.flip(grid, [AXES.index(name) for name in flip])
    return [(int(s), int(t)) for s, t in zip(grid.ravel(), moved.ravel(), strict=True)]


def swap(value, *flip):
    return lax.ppermute(value, AXES, pairs(flip))


def exchange(value):
    return lax.all_to_all(value, PLANE, split_axis=0, concat_axis=0, tiled=True)


def on_chip(kernel, operands, outs, far=(), scratch=(), far_outs=(), aliases=None):
    ins = [
        pltpu.with_memory_space_constraint(x, pltpu.HBM if k in far else pltpu.VMEM) for k, x in enumerate(operands)
    ]
    return pl.pallas_call(
        kernel,
        in_specs=[FAR if k in far else NEAR for k in range(len(ins))],
        out_specs=[FAR if k in far_outs else NEAR for k in range(len(outs))],
        out_shape=[
            jax.ShapeDtypeStruct(*out) if k in far_outs else pltpu.VMEM(*out) for k, out in enumerate(outs)
        ],
        scratch_shapes=list(scratch),
        input_output_aliases=aliases or {},
        compiler_params=pltpu.CompilerParams(vmem_limit_bytes=GRANT),
    )(*ins)


def columns_of(ref, proj, k, side):
    return ref.at[proj, :, pl.ds(pl.multiple_of((2 * k + side) * WIDTH, WIDTH), WIDTH)]


def fetch(deltas, other_core, kept):
    _, rows, columns = deltas.shape
    blocks = columns // (2 * WIDTH)

    def kernel(src, out, sem):
        proj = 1 - index("c") if other_core else index("c")
        side = kept_side() if kept else 1 - kept_side()

        def start(k, carry):
            pltpu.make_async_copy(columns_of(src, proj, k, side), out.at[k], sem).start()
            return carry

        lax.fori_loop(0, blocks, start, 0, unroll=4)
        pltpu.make_async_copy(out, out, sem).wait()

    out = ((blocks, rows, WIDTH), deltas.dtype)
    return on_chip(kernel, [deltas], [out], far=(0,), scratch=[pltpu.SemaphoreType.DMA])[0]


def add(*values):
    def kernel(*refs):
        *ins, out = refs

        def body(k, carry):
            total = ins[0][k].astype(jnp.float32)
            for ref in ins[1:]:
                total += ref[k].astype(jnp.float32)
            out[k] = total.astype(out.dtype)
            return carry

        lax.fori_loop(0, out.shape[0], body, 0, unroll=4)

    return on_chip(kernel, values, [(values[0].shape, values[0].dtype)])[0]


def part_rows(spread):
    def kernel(src, over, across, beside):
        xh, c = index("xh"), index("c")
        over[...] = src[1 - xh, c]
        across[...] = src[1 - xh, 1 - c]
        beside[...] = src[xh, 1 - c]

    out = (spread.shape[2:], spread.dtype)
    return on_chip(kernel, [spread], [out, out, out])


def update(spread, over, across, beside, master, momentum):
    count, rows, _ = over.shape

    def kernel(spread_ref, over_ref, across_ref, beside_ref, m_ref, v_ref, mo_ref, vo_ref, *outs):
        xh, c, xl = index("xh"), index("c"), index("xl")
        for p, s, src in ((0, 0, spread_ref.at[xh, c]), (0, 1, over_ref), (1, 0, beside_ref), (1, 1, across_ref)):
            proj, side, dst = jnp.bitwise_xor(c, p), jnp.bitwise_xor(xl, s), outs[2 * p + s]

            def body(k, carry, src=src, dst=dst, proj=proj, side=side):
                at = pl.ds(pl.multiple_of((2 * k + side) * rows, rows), rows)
                outer = src[k].astype(jnp.float32) * 0.25
                velocity = 0.9 * v_ref[proj, at, :] + outer
                updated = m_ref[proj, at, :] - 0.7 * (outer + 0.9 * velocity)
                vo_ref[proj, at, :] = velocity
                mo_ref[proj, at, :] = updated
                dst[k] = updated.astype(dst.dtype)
                return carry

            lax.fori_loop(0, count, body, 0, unroll=2)

    whole, piece = (master.shape, master.dtype), (over.shape, over.dtype)
    operands = [spread, over, across, beside, master, momentum]
    return on_chip(kernel, operands, [whole, whole, piece, piece, piece, piece])


def store(first, second):
    def kernel(first_ref, second_ref, first_out, second_out, sems):
        copies = [
            pltpu.make_async_copy(first_ref, first_out, sems.at[0]),
            pltpu.make_async_copy(second_ref, second_out, sems.at[1]),
        ]
        for copy in copies:
            copy.start()
        for copy in copies:
            copy.wait()

    out = (first.shape, first.dtype)
    return on_chip(kernel, [first, second], [out, out], far_outs=(0, 1), scratch=[pltpu.SemaphoreType.DMA((2,))])


def join_rows(own, over, across, beside):
    def kernel(own_ref, over_ref, across_ref, beside_ref, out):
        xh, c = index("xh"), index("c")
        out[xh, c] = own_ref[...]
        out[1 - xh, c] = over_ref[...]
        out[1 - xh, 1 - c] = across_ref[...]
        out[xh, 1 - c] = beside_ref[...]

    return on_chip(kernel, [own, over, across, beside], [((2, 2, *own.shape), own.dtype)])[0]


def place(pieces, into=None):
    rows = pieces[0][0].shape[1]
    count = len(pieces)

    def kernel(*refs):
        ins, out, sems = refs[:count], refs[-2], refs[-1]
        for j, (src, (_, first, other, kept)) in enumerate(zip(ins, pieces, strict=True)):
            proj = 1 - index("c") if other else index("c")
            side = kept_side() if kept else 1 - kept_side()

            def start(k, carry, j=j, src=src, first=first, proj=proj, side=side):
                pltpu.make_async_copy(src.at[k], columns_of(out, proj, first + k, side), sems.at[j]).start()
                return carry

            lax.fori_loop(0, src.shape[0], start, 0, unroll=4)
        for j, src in enumerate(ins):
            pltpu.make_async_copy(src, src, sems.at[j]).wait()

    operands = [piece[0] for piece in pieces] + ([] if into is None else [into])
    return on_chip(
        kernel,
        operands,
        [((2, rows, COLUMNS), operands[0].dtype)],
        far=(count,),
        far_outs=(0,),
        scratch=[pltpu.SemaphoreType.DMA((count,))],
        aliases=None if into is None else {count: 0},
    )[0]


def on_device(deltas, master, momentum):
    return step(deltas[0], master, momentum)


def across_rows(over, across, beside):
    return swap(over, "xh", "xl"), swap(across, "xh", "xl", "c"), swap(beside, "c")


def step(local, master, momentum):
    theirs = swap(fetch(local, True, False), "c")
    sent = swap(add(fetch(local, False, False), theirs), "xh")
    theirs = swap(fetch(local, True, True), "c")
    mine = fetch(local, False, True)
    summed = add(mine, theirs, sent)

    spread = exchange(summed)
    spread = spread.reshape(2, 2, -1, *spread.shape[1:])
    moved = across_rows(*part_rows(spread))
    updated, velocity, own, over, beside, across = update(spread, *moved, master, momentum)

    moved = across_rows(over, across, beside)
    updated, velocity = store(updated, velocity)
    kept = exchange(join_rows(own, *moved).reshape(summed.shape))
    early, late = swap(kept[:CUT], "xh"), swap(kept[CUT:], "xh")
    pieces = [(kept, 0, False, True), (swap(kept, "c"), 0, True, True)]
    params = place(pieces)
    early, params = lax.optimization_barrier((early, params))
    params = place([(early, 0, False, False), (swap(early, "c"), 0, True, False)], params)
    params = place([(late, CUT, False, False), (swap(late, "c"), CUT, True, False)], params)
    return updated, velocity, params


def solution(mesh):
    parts = Mesh(mesh.devices.reshape(SIZES), AXES)
    return jax.shard_map(
        on_device,
        mesh=parts,
        in_specs=(P(REPLICA, None, FSDP, None), P(None, REPLICA, FSDP), P(None, REPLICA, FSDP)),
        out_specs=(P(None, REPLICA, FSDP), P(None, REPLICA, FSDP), P(None, FSDP, None)),
        check_vma=False,
    )
```

```python
import jax
import jax.numpy as jnp
import numpy as np
from jax import lax
from jax.experimental import pallas as pl
from jax.experimental.pallas import tpu as pltpu
from jax.sharding import Mesh
from jax.sharding import PartitionSpec as P


AXES = ("xh", "c", "zh", "zm", "z0", "y", "xl")
SIZES = (2, 2, 2, 2, 2, 4, 2)
PLANE = ("zh", "zm", "z0", "y")
REPLICA = ("xh", "c")
FSDP = ("zh", "zm", "z0", "y", "xl")
WIDTH = 256
COLUMNS = 64 * WIDTH
CUT = 24
GRANT = 8 << 20


NEAR = pl.BlockSpec(memory_space=pltpu.VMEM)
FAR = pl.BlockSpec(memory_space=pltpu.HBM)


def index(*names):
    total = lax.axis_index(names[0])
    for name in names[1:]:
        total = jnp.bitwise_xor(total, lax.axis_index(name))
    return total


def kept_side():
    return index("xl", "xh", "zh")


def pairs(flip):
    grid = np.arange(np.prod(SIZES)).reshape(SIZES)
    moved = np.flip(grid, [AXES.index(name) for name in flip])
    return [(int(s), int(t)) for s, t in zip(grid.ravel(), moved.ravel(), strict=True)]


def swap(value, *flip):
    return lax.ppermute(value, AXES, pairs(flip))


def exchange(value):
    return lax.all_to_all(value, PLANE, split_axis=0, concat_axis=0, tiled=True)


def on_chip(kernel, operands, outs, far=(), scratch=(), far_outs=(), aliases=None):
    ins = [
        pltpu.with_memory_space_constraint(x, pltpu.HBM if k in far else pltpu.VMEM) for k, x in enumerate(operands)
    ]
    return pl.pallas_call(
        kernel,
        in_specs=[FAR if k in far else NEAR for k in range(len(ins))],
        out_specs=[FAR if k in far_outs else NEAR for k in range(len(outs))],
        out_shape=[
            jax.ShapeDtypeStruct(*out) if k in far_outs else pltpu.VMEM(*out) for k, out in enumerate(outs)
        ],
        scratch_shapes=list(scratch),
        input_output_aliases=aliases or {},
        compiler_params=pltpu.CompilerParams(vmem_limit_bytes=GRANT),
    )(*ins)


def columns_of(ref, proj, k, side):
    return ref.at[proj, :, pl.ds(pl.multiple_of((2 * k + side) * WIDTH, WIDTH), WIDTH)]


def fetch(deltas, other_core, kept):
    _, rows, columns = deltas.shape
    blocks = columns // (2 * WIDTH)

    def kernel(src, out, sem):
        proj = 1 - index("c") if other_core else index("c")
        side = kept_side() if kept else 1 - kept_side()

        def start(k, carry):
            pltpu.make_async_copy(columns_of(src, proj, k, side), out.at[k], sem).start()
            return carry

        lax.fori_loop(0, blocks, start, 0, unroll=8)
        pltpu.make_async_copy(out, out, sem).wait()

    out = ((blocks, rows, WIDTH), deltas.dtype)
    return on_chip(kernel, [deltas], [out], far=(0,), scratch=[pltpu.SemaphoreType.DMA])[0]


def add(*values):
    def kernel(*refs):
        *ins, out = refs

        def body(k, carry):
            total = ins[0][k].astype(jnp.float32)
            for ref in ins[1:]:
                total += ref[k].astype(jnp.float32)
            out[k] = total.astype(out.dtype)
            return carry

        lax.fori_loop(0, out.shape[0], body, 0, unroll=8)

    return on_chip(kernel, values, [(values[0].shape, values[0].dtype)])[0]


def part_rows(spread):
    def kernel(src, over, across, beside):
        xh, c = index("xh"), index("c")
        over[...] = src[1 - xh, c]
        across[...] = src[1 - xh, 1 - c]
        beside[...] = src[xh, 1 - c]

    out = (spread.shape[2:], spread.dtype)
    return on_chip(kernel, [spread], [out, out, out])


def update(spread, over, across, beside, master, momentum):
    count, rows, _ = over.shape

    def kernel(spread_ref, over_ref, across_ref, beside_ref, m_ref, v_ref, mo_ref, vo_ref, *outs):
        xh, c, xl = index("xh"), index("c"), index("xl")
        for p, s, src in ((0, 0, spread_ref.at[xh, c]), (0, 1, over_ref), (1, 0, beside_ref), (1, 1, across_ref)):
            proj, side, dst = jnp.bitwise_xor(c, p), jnp.bitwise_xor(xl, s), outs[2 * p + s]

            def body(k, carry, src=src, dst=dst, proj=proj, side=side):
                at = pl.ds(pl.multiple_of((2 * k + side) * rows, rows), rows)
                outer = src[k].astype(jnp.float32) * 0.25
                velocity = 0.9 * v_ref[proj, at, :] + outer
                updated = m_ref[proj, at, :] - 0.7 * (outer + 0.9 * velocity)
                vo_ref[proj, at, :] = velocity
                mo_ref[proj, at, :] = updated
                dst[k] = updated.astype(dst.dtype)
                return carry

            lax.fori_loop(0, count, body, 0, unroll=4)

    whole, piece = (master.shape, master.dtype), (over.shape, over.dtype)
    operands = [spread, over, across, beside, master, momentum]
    return on_chip(kernel, operands, [whole, whole, piece, piece, piece, piece])


def store(first, second):
    def kernel(first_ref, second_ref, first_out, second_out, sems):
        copies = [
            pltpu.make_async_copy(first_ref, first_out, sems.at[0]),
            pltpu.make_async_copy(second_ref, second_out, sems.at[1]),
        ]
        for copy in copies:
            copy.start()
        for copy in copies:
            copy.wait()

    out = (first.shape, first.dtype)
    return on_chip(kernel, [first, second], [out, out], far_outs=(0, 1), scratch=[pltpu.SemaphoreType.DMA((2,))])


def join_rows(own, over, across, beside):
    def kernel(own_ref, over_ref, across_ref, beside_ref, out):
        xh, c = index("xh"), index("c")
        out[xh, c] = own_ref[...]
        out[1 - xh, c] = over_ref[...]
        out[1 - xh, 1 - c] = across_ref[...]
        out[xh, 1 - c] = beside_ref[...]

    return on_chip(kernel, [own, over, across, beside], [((2, 2, *own.shape), own.dtype)])[0]


def place(pieces, into=None):
    rows = pieces[0][0].shape[1]
    count = len(pieces)

    def kernel(*refs):
        ins, out, sems = refs[:count], refs[-2], refs[-1]
        for j, (src, (_, first, other, kept)) in enumerate(zip(ins, pieces, strict=True)):
            proj = 1 - index("c") if other else index("c")
            side = kept_side() if kept else 1 - kept_side()

            def start(k, carry, j=j, src=src, first=first, proj=proj, side=side):
                pltpu.make_async_copy(src.at[k], columns_of(out, proj, first + k, side), sems.at[j]).start()
                return carry

            lax.fori_loop(0, src.shape[0], start, 0, unroll=8)
        for j, src in enumerate(ins):
            pltpu.make_async_copy(src, src, sems.at[j]).wait()

    operands = [piece[0] for piece in pieces] + ([] if into is None else [into])
    return on_chip(
        kernel,
        operands,
        [((2, rows, COLUMNS), operands[0].dtype)],
        far=(count,),
        far_outs=(0,),
        scratch=[pltpu.SemaphoreType.DMA((count,))],
        aliases=None if into is None else {count: 0},
    )[0]


def on_device(deltas, master, momentum):
    return step(deltas[0], master, momentum)


def across_rows(over, across, beside):
    return swap(over, "xh", "xl"), swap(across, "xh", "xl", "c"), swap(beside, "c")


def step(local, master, momentum):
    theirs = swap(fetch(local, True, False), "c")
    sent = swap(add(fetch(local, False, False), theirs), "xh")
    theirs = swap(fetch(local, True, True), "c")
    mine = fetch(local, False, True)
    summed = add(mine, theirs, sent)

    spread = exchange(summed)
    spread = spread.reshape(2, 2, -1, *spread.shape[1:])
    moved = across_rows(*part_rows(spread))
    updated, velocity, own, over, beside, across = update(spread, *moved, master, momentum)

    moved = across_rows(over, across, beside)
    updated, velocity = store(updated, velocity)
    kept = exchange(join_rows(own, *moved).reshape(summed.shape))
    early, late = swap(kept[:CUT], "xh"), swap(kept[CUT:], "xh")
    pieces = [(kept, 0, False, True), (swap(kept, "c"), 0, True, True)]
    params = place(pieces)
    early, params = lax.optimization_barrier((early, params))
    params = place([(early, 0, False, False), (swap(early, "c"), 0, True, False)], params)
    params = place([(late, CUT, False, False), (swap(late, "c"), CUT, True, False)], params)
    return updated, velocity, params


def solution(mesh):
    parts = Mesh(mesh.devices.reshape(SIZES), AXES)
    return jax.shard_map(
        on_device,
        mesh=parts,
        in_specs=(P(REPLICA, None, FSDP, None), P(None, REPLICA, FSDP), P(None, REPLICA, FSDP)),
        out_specs=(P(None, REPLICA, FSDP), P(None, REPLICA, FSDP), P(None, FSDP, None)),
        check_vma=False,
    )
```
